512 devices in a mesh: section: 8 (over z), row: 16 (over y, core), col: 4 (over x).
Axes of the slice: x: 4, y: 8, z: 8, core: 2. Of those that a mesh axis runs over, the one named last changes fastest.
Arguments:
- image: bfloat16 [128, 256, 1024], P('section', 'row', 'col'), may hold values from -6 to 6
- conv_kernel: float32 [7, 7, 1024], P(None, None, 'col'), may hold values from -0.875 to 0.875
- norm_gain: float32 [1024], P('col'), may hold values from 0.1 to 1.9
- w_in: bfloat16 [1024, 4096], P('row', 'col'), may hold values from -0.1875 to 0.1875
- w_out: bfloat16 [4096, 1024], P('row', 'col'), may hold values from -0.09375 to 0.09375
- upstream: bfloat16 [128, 256, 1024], P('section', 'row', 'col'), may hold values from -6 to 6
Outputs:
- output: bfloat16 [128, 256, 1024], P('section', 'row', 'col')
- image_grad: float32 [128, 256, 1024], P('section', 'row', 'col')
The draws below stay inside these ranges and needn't reach their ends.
All inputs are finite; a program needn't handle non-finite values.
Results may differ from the reference program's by a relative error of at most 0.0095.
Values may be sent and summed in bfloat16 or wider, within the bound.
A program may use at most 64 MiB of HBM per device.

```python
import math
import jax
import jax.numpy as jnp
from jax import lax

C = 1024
HID = 4096
KERNEL = 7
NLAT = 128
NLON = 256
N_COL = 4


def levels(rng, shape, shards, smallest, high):
    gain, own = 1.0, jax.random.fold_in(rng, 6)
    for axis_at, shards_of in shards:
        steps = jnp.exp(jax.random.uniform(jax.random.fold_in(own, axis_at), (shards_of,), jnp.float32, smallest / len(shards), high / len(shards)))
        gain = gain * jnp.repeat(steps, shape[axis_at] // shards_of).reshape([-1 if axis == axis_at else 1 for axis in range(len(shape))])
    return gain


def normal_values(own_key, shape, scale, bound, pieces=(), held_as=jnp.bfloat16):
    drawn = jax.random.normal(own_key, shape, jnp.float32) * scale
    if len(pieces) > 0:
        drawn = levels(own_key, shape, pieces, -0.22, 0.18) * drawn
    return jnp.clip(drawn, min=-bound, max=bound).astype(held_as)


def setup_inputs(seed: int = 0) -> dict:
    keys = jax.random.split(jax.random.key(seed), 7)
    return {
        "image": normal_values(keys[0], (NLAT, NLON, C), 1.0, 6.0, ((0, 8), (1, 16), (2, 4))),
        "conv_kernel": normal_values(keys[1], (KERNEL, KERNEL, C), (KERNEL * KERNEL) ** -0.5, 0.875, ((2, 4),), jnp.float32),
        "norm_gain": jnp.clip(1.0 + 0.18 * jax.random.normal(keys[2], (C,), jnp.float32), 0.1, 1.9),
        "w_in": normal_values(keys[3], (C, HID), C ** -0.5, 0.1875, ((0, 16), (1, 4))),
        "w_out": normal_values(keys[4], (HID, C), HID ** -0.5, 0.09375, ((0, 16), (1, 4))),
        "upstream": normal_values(keys[5], (NLAT, NLON, C), 1.0, 6.0, ((0, 8), (1, 16), (2, 4))),
    }


EPSILON = 1e-06

def depthwise(padded, kernel, height, breadth, start):
    total = jnp.zeros((height, breadth, padded.shape[2]), jnp.float32)
    for row_off in range(KERNEL):
        for col_off in range(KERNEL):
            lead = start - row_off if start > 0 else row_off
            side = start - col_off if start > 0 else col_off
            total = total + padded[lead:lead + height, side:side + breadth, :] * kernel[row_off, col_off]
    return total

def gelu_slope(preact):
    return 0.5 * (1.0 + lax.erf(preact / math.sqrt(2.0))) + preact * jnp.exp(-0.5 * preact * preact) / math.sqrt(2.0 * math.pi)

def reference(image, conv_kernel, norm_gain, w_in, w_out, upstream):
    height, breadth, channels = image.shape
    margin = KERNEL // 2
    widths = ((margin, margin), (margin, margin), (0, 0))
    mixed = depthwise(jnp.pad(image.astype(jnp.float32), widths), conv_kernel, height, breadth, 0)
    centre = lax.optimization_barrier(jnp.mean(mixed, axis=-1, keepdims=True))
    centred = mixed - centre
    spread = lax.optimization_barrier(jnp.mean(centred * centred, axis=-1, keepdims=True))
    inv_std = lax.rsqrt(spread + EPSILON)
    normed = centred * inv_std
    scaled = (normed * norm_gain).astype(jnp.bfloat16).reshape(-1, channels)
    preact = jnp.dot(scaled, w_in, preferred_element_type=jnp.float32)
    hidden = jax.nn.gelu(preact, approximate=False).astype(jnp.bfloat16)
    branch = jnp.dot(hidden, w_out, preferred_element_type=jnp.float32)
    flat_image = image.reshape(-1, channels).astype(jnp.float32)
    output = (flat_image + branch).astype(jnp.bfloat16).reshape(image.shape)
    grad_flat = upstream.reshape(-1, channels)
    chan_block = channels // N_COL
    hid_block = w_in.shape[1] // N_COL
    hidden_grad = jnp.zeros(preact.shape, jnp.float32)
    for block in range(N_COL):
        lo_c = block * chan_block
        term = jnp.dot(grad_flat[:, lo_c:lo_c + chan_block], w_out[:, lo_c:lo_c + chan_block].T, preferred_element_type=jnp.float32)
        term = lax.optimization_barrier(term.astype(jnp.bfloat16))
        hidden_grad = hidden_grad + term.astype(jnp.float32)
    act_grad = (hidden_grad * gelu_slope(preact)).astype(jnp.bfloat16)
    feature_grad = jnp.zeros(scaled.shape, jnp.float32)
    for block in range(N_COL):
        lo_h = block * hid_block
        term = jnp.dot(act_grad[:, lo_h:lo_h + hid_block], w_in[:, lo_h:lo_h + hid_block].T, preferred_element_type=jnp.float32)
        term = lax.optimization_barrier(term.astype(jnp.bfloat16))
        feature_grad = feature_grad + term.astype(jnp.float32)
    normed_grad = feature_grad.reshape(image.shape) * norm_gain
    first = lax.optimization_barrier(jnp.mean(normed_grad, axis=-1, keepdims=True))
    second = lax.optimization_barrier(jnp.mean(normed_grad * normed, axis=-1, keepdims=True))
    mixed_grad = inv_std * (normed_grad - first - normed * second)
    grad_pad = jnp.pad(mixed_grad, widths)
    image_grad = upstream.astype(jnp.float32) + depthwise(grad_pad, conv_kernel, height, breadth, 2 * margin)
    return (output, image_grad)
```

```python
import functools
import math

import jax
import jax.numpy as jnp
from jax import lax
from jax.experimental import pallas as pl
from jax.experimental.pallas import tpu as pltpu
from jax.sharding import PartitionSpec as P

KERNEL = 7
EPSILON = 1e-06
MESH = pl.DeviceIdType.MESH
F32, BF16 = jnp.float32, jnp.bfloat16
EDGE = 8


def dot_nn(left, right):
    return lax.dot_general(left, right, (((1,), (0,)), ((), ())), preferred_element_type=F32)


def dot_nt(left, right):
    return lax.dot_general(left, right, (((1,), (1,)), ((), ())), preferred_element_type=F32)


def body(
    image, kern, gain, w_in, w_out, up, out, igrad,
    hlon, hlat, hcor, pad, mix, feat, stat, stat2, ups, win, sl, wo, pre, gws, hb, ag,
    sums, fgs, fgr, fgo, obs, obr, obo, mgb, dinv,
    s_halo, r_halo, s_ft, r_ft, s_st, r_st, s_up, r_up, s_wl, s_ws, s_wp, r_w,
    s_sl, r_sl, s_wx, r_wx, s_zl, s_zs, s_zp, r_z, s_fg, r_fg, s_s2, r_s2, s_ob, r_ob, s_loc,
):
    nz, nr, nx = lax.axis_size("section"), lax.axis_size("row"), lax.axis_size("col")
    ny = nr // 2
    long, short = ny // 2, ny - 1 - ny // 2
    zlong, zshort = nz // 2, nz - 1 - nz // 2
    z, r, x = lax.axis_index("section"), lax.axis_index("row"), lax.axis_index("col")
    y, c = lax.div(r, 2), lax.rem(r, 2)
    turn = 1 - 2 * c
    cells = 256

    def at_y(d):
        return lax.rem(y + d + ny, ny)

    def at_z(d):
        return lax.rem(z + d + nz, nz)

    def at_x(d):
        return lax.rem(x + d, nx)

    def row_dev(yy, cc):
        return {"row": 2 * yy + cc}

    partner = row_dev(y, 1 - c)

    def send(src, dst, ssem, rsem, dev):
        return pltpu.make_async_remote_copy(
            src_ref=src, dst_ref=dst, send_sem=ssem, recv_sem=rsem, device_id=dev,
            device_id_type=MESH,
        )

    def got(ref, rsem):
        send(ref, ref, s_loc.at[0], rsem, partner).wait_recv()

    around = [(dz, dr) for dz in (-1, 0, 1) for dr in (-1, 0, 1) if (dz, dr) != (0, 0)]

    stat[...] = jnp.zeros(stat.shape, F32)
    stat2[...] = jnp.zeros(stat2.shape, F32)

    barrier = pltpu.get_barrier_semaphore()
    greeted = 0
    for dz, dr in around:
        pl.semaphore_signal(
            barrier, inc=1, device_id={"section": at_z(dz), "row": lax.rem(r + dr + nr, nr)},
            device_id_type=MESH,
        )
        greeted += 1
    for d in range(1, nx):
        pl.semaphore_signal(barrier, inc=1, device_id={"col": at_x(d)}, device_id_type=MESH)
        greeted += 1
    for d in range(1, ny):
        pl.semaphore_signal(barrier, inc=1, device_id=row_dev(at_y(d), c), device_id_type=MESH)
        greeted += 1
    for d in (-1, 1):
        pl.semaphore_signal(barrier, inc=1, device_id={"section": at_z(d)}, device_id_type=MESH)
        greeted += 1
    pl.semaphore_signal(barrier, inc=1, device_id=partner, device_id_type=MESH)
    greeted += 1
    pl.semaphore_wait(barrier, greeted)

    def lat_of(dz, ref_lats):
        return pl.ds(ref_lats - 3, 3) if dz > 0 else pl.ds(0, 3)

    def lon_of(dr):
        return pl.ds(16 - EDGE, EDGE) if dr > 0 else pl.ds(0, EDGE)

    def halo_slot(p, dz, dr):
        if dz == 0:
            return hlon.at[p, 0 if dr > 0 else 1]
        if dr == 0:
            return hlat.at[p, 0 if dz > 0 else 1]
        return hcor.at[p, (0 if dz > 0 else 2) + (0 if dr > 0 else 1)]

    def inside(dz, dr):
        zz, rr = z + dz, r + dr
        return jnp.logical_and(
            jnp.logical_and(zz >= 0, zz < nz), jnp.logical_and(rr >= 0, rr < nr)
        )

    def halo_copy(p, n, ref):
        dz, dr = around[n]
        if dz == 0:
            src = ref.at[:, lon_of(dr), :]
        elif dr == 0:
            src = ref.at[lat_of(dz, 16)]
        else:
            src = ref.at[lat_of(dz, 16), lon_of(dr), :]
        dev = {"section": at_z(dz), "row": lax.rem(r + dr + nr, nr)}
        return send(src, halo_slot(p, dz, dr), s_halo.at[p, n], r_halo.at[p, n], dev)

    def halo_start(p, ref):
        for n, (dz, dr) in enumerate(around):
            @pl.when(inside(dz, dr))
            def _():
                halo_copy(p, n, ref).start()

    def halo_sent(p, ref):
        for n, (dz, dr) in enumerate(around):
            @pl.when(inside(dz, dr))
            def _():
                halo_copy(p, n, ref).wait_send()

    def halo_take(p):
        for n, (dz, dr) in enumerate(around):
            lats = pl.ds(3, 16) if dz == 0 else (pl.ds(0, 3) if dz > 0 else pl.ds(19, 3))
            lons = pl.ds(8, 16) if dr == 0 else (pl.ds(0, 8) if dr > 0 else pl.ds(24, 8))
            slot = halo_slot(p, dz, dr)
            shape = (16 if dz == 0 else 3, 16 if dr == 0 else 8, 256)

            @pl.when(inside(-dz, -dr))
            def _():
                got(slot, r_halo.at[p, n])
                pad[lats, lons, :] = slot[...].astype(F32)

            @pl.when(jnp.logical_not(inside(-dz, -dr)))
            def _():
                pad[lats, lons, :] = jnp.zeros(shape, F32)

    def conv(flip, emit):
        def group(g, carry):
            i0 = g * 4
            acc = [jnp.zeros((16, 256), F32) for _ in range(4)]
            for b in range(KERNEL):
                rows = [pad[i0 + t, pl.ds(5 + b, 16), :] for t in range(10)]
                for a in range(KERNEL):
                    tap = kern[KERNEL - 1 - a, KERNEL - 1 - b, :] if flip else kern[a, b, :]
                    tap = tap.reshape(1, 256)
                    for q in range(4):
                        acc[q] = acc[q] + rows[q + a] * tap
            for q in range(4):
                emit(i0 + q, acc[q])
            return carry

        lax.fori_loop(0, 4, group, 0)

    def win_send(far, t):
        owner = at_y(-turn * t) if far else at_y(turn * t)
        dev = row_dev(at_y(turn) if far else at_y(-turn), c)
        slot = 2 * owner + c
        src = w_in if t == 0 else win.at[slot]
        return send(src, win.at[slot], (s_wl if far else s_ws).at[t], r_w.at[slot], dev)

    def win_share(t, owner):
        slot = 2 * owner + c
        src = w_in if t == 0 else win.at[slot]
        return send(src, win.at[slot], s_wp.at[t], r_w.at[slot], partner)

    def win_relay(d):
        if d <= long:
            owner = at_y(-turn * d)
            got(win.at[2 * owner + c], r_w.at[2 * owner + c])
            if d < long:
                win_send(True, d).start()
            win_share(d, owner).start()
        if d <= short:
            owner = at_y(turn * d)
            got(win.at[2 * owner + c], r_w.at[2 * owner + c])
            if d < short:
                win_send(False, d).start()
            win_share(long + d, owner).start()

    def zone(zz, cc):
        return wo.at[:, :, cc, zz]

    def wo_send(far, t):
        owner = at_z(-turn * t) if far else at_z(turn * t)
        dev = {"section": at_z(turn) if far else at_z(-turn)}
        ref = zone(owner, c)
        return send(ref, ref, (s_zl if far else s_zs).at[t], r_z.at[2 * owner + c], dev)

    def wo_share(t, owner):
        ref = zone(owner, c)
        return send(ref, ref, s_zp.at[t], r_z.at[2 * owner + c], partner)

    def wo_relay(d):
        if d <= zlong:
            owner = at_z(-turn * d)
            got(zone(owner, c), r_z.at[2 * owner + c])
            if d < zlong:
                wo_send(True, d).start()
            wo_share(d, owner).start()
        if d <= zshort:
            owner = at_z(turn * d)
            got(zone(owner, c), r_z.at[2 * owner + c])
            if d < zshort:
                wo_send(False, d).start()
            wo_share(zlong + d, owner).start()

    halo_start(0, image)
    win_send(True, 0).start()
    win_send(False, 0).start()
    win_share(0, y).start()

    my_rows = w_out.at[pl.ds(pl.multiple_of(z * 32, 32), 32), :]

    def slice_send(d):
        return send(my_rows, sl.at[y], s_sl.at[d - 1], r_sl.at[y], row_dev(at_y(d), c))

    def to_col(src, dst, ssem, rsem, d):
        return send(src, dst, ssem.at[d - 1], rsem.at[x], {"col": at_x(d)})

    for d in range(1, ny):
        slice_send(d).start()
    for d in range(1, nx):
        to_col(up, ups.at[x], s_up, r_up, d).start()
    local = [
        pltpu.make_async_copy(w_in, win.at[r], s_loc.at[1]),
        pltpu.make_async_copy(my_rows, sl.at[y], s_loc.at[2]),
        pltpu.make_async_copy(up, ups.at[x], s_loc.at[3]),
    ]
    for copy in local:
        copy.start()

    pad[pl.ds(3, 16), pl.ds(8, 16), :] = image[...].astype(F32)
    halo_take(0)
    win_relay(1)

    def keep(i, value):
        mix[i] = value

    conv(False, keep)

    flat = mix[...].reshape(cells, 256)
    mean_own = jnp.sum(flat, axis=-1, keepdims=True) * (1.0 / 256)
    centred = flat - mean_own
    square = jnp.sum(centred * centred, axis=-1, keepdims=True)
    g_row = gain[...]
    feat[x, pl.ds(0, cells), :] = (centred * g_row).astype(BF16)
    g_high = g_row.astype(BF16).astype(F32)
    tail = lax.broadcasted_iota(jnp.int32, (16, 256), 0)
    feat[x, pl.ds(cells, 16), :] = jnp.where(
        tail == 0, g_high, jnp.where(tail == 1, g_row - g_high, 0.0)
    ).astype(BF16)
    lane = lax.broadcasted_iota(jnp.int32, (cells, 128), 1)

    def as_rows(first, second):
        both = jnp.where(lane == 0, first, jnp.where(lane == 1, second, 0.0))
        return both.T[0:8, :]

    rows_own = as_rows(mean_own, square)
    s_rows = rows_own
    stat_own = pl.ds(pl.multiple_of(x * 8, 8), 8)
    stat[stat_own, :] = s_rows
    for d in range(1, nx):
        to_col(stat.at[stat_own, :], stat.at[stat_own, :], s_st, r_st, d).start()
        to_col(feat.at[x], feat.at[x], s_ft, r_ft, d).start()

    for copy in local:
        copy.wait()
    for d in range(1, ny):
        got(sl.at[at_y(d)], r_sl.at[at_y(d)])

    def cross(d):
        dest = at_x(d)
        return send(
            sl.at[pl.ds(2 * dest, 2)], wo.at[x, :, c, z], s_wx.at[d - 1], r_wx.at[x],
            {"col": dest},
        )

    for d in range(1, nx):
        cross(d).start()
    mine = pltpu.make_async_copy(sl.at[pl.ds(2 * x, 2)], wo.at[x, :, c, z], s_loc.at[4])
    mine.start()
    win_relay(2)
    mine.wait()
    for d in range(1, nx):
        got(wo.at[at_x(d), :, c, z], r_wx.at[at_x(d)])
    wo_send(True, 0).start()
    wo_send(False, 0).start()
    wo_share(0, z).start()
    for d in range(3, long + 1):
        win_relay(d)

    for d in range(1, nx):
        k = at_x(d)
        got(stat.at[pl.ds(pl.multiple_of(k * 8, 8), 8), :], r_st.at[k])
        got(feat.at[k], r_ft.at[k])
    wo_relay(1)
    for yy in range(ny):
        slot = 2 * yy + 1 - c
        got(win.at[slot], r_w.at[slot])

    columns = stat[...].T
    means = [columns[:, 8 * k : 8 * k + 1] for k in range(nx)]
    centre = (means[0] + means[1] + means[2] + means[3]) * 0.25
    shifts = [m - centre for m in means]
    total = columns[:, 1:2] + columns[:, 9:10] + columns[:, 17:18] + columns[:, 25:26]
    spread = total + 256.0 * (
        shifts[0] * shifts[0] + shifts[1] * shifts[1] + shifts[2] * shifts[2]
        + shifts[3] * shifts[3]
    )
    inv_std = lax.rsqrt(spread * (1.0 / 1024) + EPSILON)
    for k in range(nx):
        dinv[k] = jnp.broadcast_to(shifts[k] * inv_std, (cells, 128))
    dinv[4] = jnp.broadcast_to(inv_std, (cells, 128))
    dinv[5] = jnp.broadcast_to(centre, (cells, 128))

    def wide(n):
        half = dinv[n]
        return jnp.concatenate([half, half], axis=1)

    def first_product(n, carry):
        cols = pl.ds(pl.multiple_of(n * 256, 256), 256)
        acc = jnp.zeros((cells, 256), F32)
        shift = jnp.zeros((cells, 256), F32)
        gsum = jnp.zeros((1, 256), F32)
        for k in range(nx):
            block = win[4 * k : 4 * k + 4, :, cols].reshape(256, 256)
            part = dot_nn(feat[k], block)
            acc = acc + part[:cells]
            row = part[cells : cells + 1] + part[cells + 1 : cells + 2]
            shift = shift + wide(k) * row
            gsum = gsum + row
        pre[:, cols] = acc * wide(4) + shift
        gws[:, cols] = jnp.broadcast_to(gsum, (8, 256))
        return carry

    lax.fori_loop(0, 4, first_product, 0)

    for d in range(2, zlong + 1):
        wo_relay(d)
    for d in range(1, nx):
        got(ups.at[at_x(d)], r_up.at[at_x(d)])
    for zz in range(nz):
        got(zone(zz, 1 - c), r_z.at[2 * zz + 1 - c])

    sums[...] = jnp.zeros(sums.shape, F32)

    def activation(n, carry):
        cols = pl.ds(pl.multiple_of(n * 256, 256), 256)
        grad = jnp.zeros((cells, 256), F32)
        for k in range(nx):
            block = wo[k, lax.div(n, 2), lax.rem(n, 2)].reshape(256, 256)
            grad = grad + dot_nt(ups[k].reshape(cells, 256), block)
        value = pre[:, cols]
        phi = 0.5 * (1.0 + lax.erf(value * (1.0 / math.sqrt(2.0))))
        slope = phi + value * jnp.exp(-0.5 * value * value) * (1.0 / math.sqrt(2.0 * math.pi))
        hb[:, cols] = (value * phi).astype(BF16)
        act = (grad * slope).astype(BF16)
        ag[:, cols] = act
        actf = act.astype(F32)
        one = actf * gws[0:1, cols]
        two = actf * value
        sums[0] += one[:, :128] + one[:, 128:]
        sums[1] += two[:, :128] + two[:, 128:]
        return carry

    lax.fori_loop(0, 4, activation, 0)

    def win_block(k):
        return win[pl.ds(pl.multiple_of(k * 4, 4), 4)].reshape(256, 1024)

    stat2[stat_own, :] = as_rows(
        jnp.sum(sums[0], axis=-1, keepdims=True), jnp.sum(sums[1], axis=-1, keepdims=True)
    )
    for d in range(1, nx):
        to_col(stat2.at[stat_own, :], stat2.at[stat_own, :], s_s2, r_s2, d).start()

    def fg_copy(d):
        return to_col(fgs.at[d - 1], fgr.at[x], s_fg, r_fg, d)

    def ob_copy(d):
        return to_col(obs.at[d - 1], obr.at[x], s_ob, r_ob, d)

    for d in (2, 1, 3):
        fgs[d - 1] = dot_nt(ag[...], win_block(at_x(d))).astype(BF16)
        fg_copy(d).start()
    fgo[...] = dot_nt(ag[...], win_block(x))
    for d in (2, 1, 3):
        obs[d - 1] = dot_nn(hb[...], wo[at_x(d)].reshape(1024, 256)).astype(BF16)
        ob_copy(d).start()
    obo[...] = dot_nn(hb[...], wo[x].reshape(1024, 256))

    for d in range(1, nx):
        k = at_x(d)
        got(stat2.at[pl.ds(pl.multiple_of(k * 8, 8), 8), :], r_s2.at[k])
        got(fgr.at[k], r_fg.at[k])
    feature = fgo[...]
    for d in range(1, nx):
        feature = feature + fgr[at_x(d)].astype(F32)
    columns2 = stat2[...].T
    first = (
        columns2[:, 0:1] + columns2[:, 8:9] + columns2[:, 16:17] + columns2[:, 24:25]
    ) * (1.0 / 1024)
    second = (
        columns2[:, 1:2] + columns2[:, 9:10] + columns2[:, 17:18] + columns2[:, 25:26]
    ) * (1.0 / 1024)
    inv_wide = wide(4)
    normed = (mix[...].reshape(cells, 256) - wide(5)) * inv_wide
    mixed_grad = inv_wide * (feature * g_row - first - normed * second)
    mgb[...] = mixed_grad.astype(BF16).reshape(16, 16, 256)
    halo_start(1, mgb)
    pad[pl.ds(3, 16), pl.ds(8, 16), :] = mixed_grad.reshape(16, 16, 256)

    for d in range(1, nx):
        got(obr.at[at_x(d)], r_ob.at[at_x(d)])
    branch = obo[...]
    for d in range(1, nx):
        branch = branch + obr[at_x(d)].astype(F32)
    out[...] = (image[...].astype(F32) + branch.reshape(16, 16, 256)).astype(BF16)

    halo_take(1)

    def finish(i, value):
        igrad[i] = up[i].astype(F32) + value

    conv(True, finish)

    halo_sent(0, image)
    halo_sent(1, mgb)
    for t in range(long):
        win_send(True, t).wait_send()
    for t in range(short):
        win_send(False, t).wait_send()
    for t in range(ny):
        win_share(t, y).wait_send()
    for t in range(zlong):
        wo_send(True, t).wait_send()
    for t in range(zshort):
        wo_send(False, t).wait_send()
    for t in range(nz):
        wo_share(t, z).wait_send()
    for d in range(1, ny):
        slice_send(d).wait_send()
    for d in range(1, nx):
        to_col(up, ups.at[x], s_up, r_up, d).wait_send()
        to_col(stat.at[stat_own, :], stat.at[stat_own, :], s_st, r_st, d).wait_send()
        to_col(feat.at[x], feat.at[x], s_ft, r_ft, d).wait_send()
        to_col(stat2.at[stat_own, :], stat2.at[stat_own, :], s_s2, r_s2, d).wait_send()
        cross(d).wait_send()
        fg_copy(d).wait_send()
        ob_copy(d).wait_send()


def local(image, conv_kernel, norm_gain, w_in, w_out, upstream):
    nz, nr, nx = lax.axis_size("section"), lax.axis_size("row"), lax.axis_size("col")
    ny = nr // 2
    height, breadth, chan = image.shape
    cells = height * breadth
    vmem = pl.BlockSpec(memory_space=pltpu.VMEM)
    dma = pltpu.SemaphoreType.DMA
    scratch = [
        pltpu.VMEM((2, 2, 16, EDGE, chan), BF16),
        pltpu.VMEM((2, 2, 3, 16, chan), BF16),
        pltpu.VMEM((2, 4, 3, EDGE, chan), BF16),
        pltpu.VMEM((22, 32, chan), F32),
        pltpu.VMEM((height, breadth, chan), F32),
        pltpu.VMEM((nx, cells + 16, chan), BF16),
        pltpu.VMEM((128, cells), F32),
        pltpu.VMEM((128, cells), F32),
        pltpu.VMEM((nx, height, breadth, chan), BF16),
        pltpu.VMEM((nr, 64, 1024), BF16),
        pltpu.VMEM((ny, 32, chan), BF16),
        pltpu.VMEM((nx, 2, 2, nz, 32, chan), BF16),
        pltpu.VMEM((cells, 1024), F32),
        pltpu.VMEM((8, 1024), F32),
        pltpu.VMEM((cells, 1024), BF16),
        pltpu.VMEM((cells, 1024), BF16),
        pltpu.VMEM((2, cells, 128), F32),
        pltpu.VMEM((nx - 1, cells, chan), BF16),
        pltpu.VMEM((nx, cells, chan), BF16),
        pltpu.VMEM((cells, chan), F32),
        pltpu.VMEM((nx - 1, cells, chan), BF16),
        pltpu.VMEM((nx, cells, chan), BF16),
        pltpu.VMEM((cells, chan), F32),
        pltpu.VMEM((height, breadth, chan), BF16),
        pltpu.VMEM((6, cells, 128), F32),
        dma((2, 8)), dma((2, 8)),
        dma((nx - 1,)), dma((nx,)),
        dma((nx - 1,)), dma((nx,)),
        dma((nx - 1,)), dma((nx,)),
        dma((ny // 2,)), dma((ny // 2,)), dma((ny,)), dma((nr,)),
        dma((ny - 1,)), dma((ny,)),
        dma((nx - 1,)), dma((nx,)),
        dma((nz // 2,)), dma((nz // 2,)), dma((nz,)), dma((2 * nz,)),
        dma((nx - 1,)), dma((nx,)),
        dma((nx - 1,)), dma((nx,)),
        dma((nx - 1,)), dma((nx,)),
        dma((5,)),
    ]
    return pl.pallas_call(
        body,
        out_shape=(
            jax.ShapeDtypeStruct(image.shape, BF16),
            jax.ShapeDtypeStruct(image.shape, F32),
        ),
        in_specs=[vmem] * 6,
        out_specs=(vmem, vmem),
        scratch_shapes=scratch,
        compiler_params=pltpu.CompilerParams(
            collective_id=0, has_side_effects=True, vmem_limit_bytes=60 * 1024 * 1024
        ),
        name="block",
    )(image, conv_kernel, norm_gain.reshape(1, chan), w_in, w_out, upstream)


def solution(mesh):
    in_specs = (
        P("section", "row", "col"),
        P(None, None, "col"),
        P("col"),
        P("row", "col"),
        P("row", "col"),
        P("section", "row", "col"),
    )
    out_specs = (P("section", "row", "col"), P("section", "row", "col"))
    return jax.shard_map(local, mesh=mesh, in_specs=in_specs, out_specs=out_specs, check_vma=False)
```

```python
import functools
import math

import jax
import jax.numpy as jnp
from jax import lax
from jax.experimental import pallas as pl
from jax.experimental.pallas import tpu as pltpu
from jax.sharding import PartitionSpec as P

KERNEL = 7
EPSILON = 1e-06
MESH = pl.DeviceIdType.MESH
F32, BF16 = jnp.float32, jnp.bfloat16
EDGE = 8


def dot_nn(left, right):
    return lax.dot_general(left, right, (((1,), (0,)), ((), ())), preferred_element_type=F32)


def dot_nt(left, right):
    return lax.dot_general(left, right, (((1,), (1,)), ((), ())), preferred_element_type=F32)


def body(
    image_hbm, kern_hbm, gain_hbm, w_in, w_out, up_hbm, out, igrad,
    image, kern, gain,
    hlon, hlat, hcor, pad, mix, feat, stat, stat2, ups, win, sl, wo, pre, gws, hb, ag,
    sums, fg2, fgk, fgs, fge, fgr, fgo, ob2, obk, obs, obe, obr, obo, mgb, dinv,
    s_halo, r_halo, s_ft, r_ft, s_st, r_st, s_up, r_up, s_w, r_w, r_wp,
    s_sl, r_sl, s_wx, r_wx, s_z, r_z, r_zp, s_fg, r_fg, s_s2, r_s2, s_ob, r_ob, s_loc,
):
    nz, nr, nx = lax.axis_size("section"), lax.axis_size("row"), lax.axis_size("col")
    ny = nr // 2
    long, short = ny // 2, ny - 1 - ny // 2
    zlong, zshort = nz // 2, nz - 1 - nz // 2
    z, r, x = lax.axis_index("section"), lax.axis_index("row"), lax.axis_index("col")
    y, c = lax.div(r, 2), lax.rem(r, 2)
    turn = 1 - 2 * c
    cells, half = 256, 128

    def at_y(d):
        return lax.rem(y + d + ny, ny)

    def at_z(d):
        return lax.rem(z + d + nz, nz)

    def at_x(d):
        return lax.rem(x + d, nx)

    def row_dev(yy, cc):
        return {"row": 2 * yy + cc}

    partner = row_dev(y, 1 - c)

    def send(src, dst, ssem, rsem, dev):
        return pltpu.make_async_remote_copy(
            src_ref=src, dst_ref=dst, send_sem=ssem, recv_sem=rsem, device_id=dev,
            device_id_type=MESH,
        )

    def got(ref, rsem):
        send(ref, ref, s_loc.at[0], rsem, partner).wait_recv()

    def left_here(ref, ssem):
        send(ref, ref, ssem, s_loc.at[0], partner).wait_send()

    around = [(dz, dr) for dz in (-1, 0, 1) for dr in (-1, 0, 1) if (dz, dr) != (0, 0)]

    loads = [
        pltpu.make_async_copy(image_hbm, image, s_loc.at[5]),
        pltpu.make_async_copy(kern_hbm, kern, s_loc.at[6]),
        pltpu.make_async_copy(gain_hbm, gain, s_loc.at[7]),
    ]
    barrier = pltpu.get_barrier_semaphore()
    greeted = 0
    for dz, dr in around:
        pl.semaphore_signal(
            barrier, inc=1, device_id={"section": at_z(dz), "row": lax.rem(r + dr + nr, nr)},
            device_id_type=MESH,
        )
        greeted += 1
    for d in range(1, nx):
        pl.semaphore_signal(barrier, inc=1, device_id={"col": at_x(d)}, device_id_type=MESH)
        greeted += 1
    for d in range(1, ny):
        pl.semaphore_signal(barrier, inc=1, device_id=row_dev(at_y(d), c), device_id_type=MESH)
        greeted += 1
    for d in (-1, 1):
        pl.semaphore_signal(barrier, inc=1, device_id={"section": at_z(d)}, device_id_type=MESH)
        greeted += 1
    pl.semaphore_signal(barrier, inc=1, device_id=partner, device_id_type=MESH)
    greeted += 1
    for copy in loads:
        copy.start()
    stat[pl.ds(8 * nx, 128 - 8 * nx), :] = jnp.zeros((128 - 8 * nx, cells), F32)
    stat2[pl.ds(8 * nx, 128 - 8 * nx), :] = jnp.zeros((128 - 8 * nx, cells), F32)
    pl.semaphore_wait(barrier, greeted)

    def lat_of(dz, ref_lats):
        return pl.ds(ref_lats - 3, 3) if dz > 0 else pl.ds(0, 3)

    def lon_of(dr):
        return pl.ds(16 - EDGE, EDGE) if dr > 0 else pl.ds(0, EDGE)

    def halo_slot(p, dz, dr):
        if dz == 0:
            return hlon.at[p, 0 if dr > 0 else 1]
        if dr == 0:
            return hlat.at[p, 0 if dz > 0 else 1]
        return hcor.at[p, (0 if dz > 0 else 2) + (0 if dr > 0 else 1)]

    def inside(dz, dr):
        zz, rr = z + dz, r + dr
        return jnp.logical_and(
            jnp.logical_and(zz >= 0, zz < nz), jnp.logical_and(rr >= 0, rr < nr)
        )

    def halo_copy(p, n, ref):
        dz, dr = around[n]
        if dz == 0:
            src = ref.at[:, lon_of(dr), :]
        elif dr == 0:
            src = ref.at[lat_of(dz, 16)]
        else:
            src = ref.at[lat_of(dz, 16), lon_of(dr), :]
        dev = {"section": at_z(dz), "row": lax.rem(r + dr + nr, nr)}
        return send(src, halo_slot(p, dz, dr), s_halo.at[p], r_halo.at[p], dev)

    def halo_start(p, ref):
        for n in range(len(around)):
            halo_copy(p, n, ref).start()

    halo_bytes = win.at[pl.ds(0, 7), pl.ds(0, 16)]

    def fill(lats, lons, value):
        pad[0, lats, lons, :] = value[:, :, :128]
        pad[1, lats, lons, :] = value[:, :, 128:]

    def halo_take(p):
        got(halo_bytes, r_halo.at[p])
        for dz, dr in around:
            lats = pl.ds(3, 16) if dz == 0 else (pl.ds(0, 3) if dz > 0 else pl.ds(19, 3))
            lons = pl.ds(8, 16) if dr == 0 else (pl.ds(0, 8) if dr > 0 else pl.ds(24, 8))
            slot = halo_slot(p, dz, dr)
            value = slot[...].astype(F32)
            fill(lats, lons, jnp.where(inside(-dz, -dr), value, 0.0))

    def conv(flip, top, emit):
        def lanes(h, carry):
            cols = pl.ds(pl.multiple_of(h * 128, 128), 128)
            acc = [jnp.zeros((16, 128), F32) for _ in range(8)]
            for b in range(KERNEL):
                rows = [pad[h, top + t, pl.ds(5 + b, 16), :] for t in range(14)]
                for a in range(KERNEL):
                    at = (KERNEL - 1 - a, KERNEL - 1 - b) if flip else (a, b)
                    tap = kern[at[0], at[1] : at[1] + 1, cols]
                    for q in range(8):
                        acc[q] = acc[q] + rows[q + a] * tap
            for q in range(8):
                emit(top + q, cols, acc[q])
            return carry

        lax.fori_loop(0, 2, lanes, 0)

    def win_part(slot, j):
        return win.at[slot, pl.ds(32 * j, 32)]

    def win_from(t, slot, j):
        return w_in.at[pl.ds(32 * j, 32)] if t == 0 else win_part(slot, j)

    def win_send(far, t, j):
        owner = at_y(-turn * t) if far else at_y(turn * t)
        dev = row_dev(at_y(turn) if far else at_y(-turn), c)
        slot = 2 * owner + c
        return send(
            win_from(t, slot, j), win_part(slot, j), s_w, r_w.at[slot, j], dev,
        )

    def win_share(t, owner, j):
        slot = 2 * owner + c
        return send(
            win_from(t, slot, j), win_part(slot, j), s_w, r_wp, partner
        )

    def win_relay(d, j):
        if d <= long:
            slot = 2 * at_y(-turn * d) + c
            got(win_part(slot, j), r_w.at[slot, j])
            if d < long:
                win_send(True, d, j).start()
            win_share(d, at_y(-turn * d), j).start()
        if d <= short:
            slot = 2 * at_y(turn * d) + c
            got(win_part(slot, j), r_w.at[slot, j])
            if d < short:
                win_send(False, d, j).start()
            win_share(long + d, at_y(turn * d), j).start()

    def zone(zz, cc, j):
        return wo.at[:, j, cc, zz]

    def wo_send(far, t, j):
        owner = at_z(-turn * t) if far else at_z(turn * t)
        dev = {"section": at_z(turn) if far else at_z(-turn)}
        ref = zone(owner, c, j)
        return send(ref, ref, s_z, r_z.at[owner, j], dev)

    def wo_share(t, owner, j):
        ref = zone(owner, c, j)
        return send(ref, ref, s_z, r_zp, partner)

    def wo_relay(d, j):
        if d <= zlong:
            owner = at_z(-turn * d)
            got(zone(owner, c, j), r_z.at[owner, j])
            if d < zlong:
                wo_send(True, d, j).start()
            wo_share(d, owner, j).start()
        if d <= zshort:
            owner = at_z(turn * d)
            got(zone(owner, c, j), r_z.at[owner, j])
            if d < zshort:
                wo_send(False, d, j).start()
            wo_share(zlong + d, owner, j).start()

    right, left = {"col": at_x(1)}, {"col": at_x(nx - 1)}

    def ring_copy(src, ref, parts, ssem, rsem, n):
        part = (0, 1, 1, 0, 0, 1)[n]
        owner = x if n < 4 else (at_x(nx - 1) if n == 4 else at_x(1))
        dst = ref.at[owner, parts[part]]
        return send(
            src.at[parts[part]] if n < 4 and src is not None else dst, dst, ssem,
            rsem.at[min(n, 2)], right if n in (0, 2, 4) else left,
        )

    def ring_relay(ref, parts, ssem, rsem):
        got(ref.at[at_x(nx - 1), parts[0]], rsem.at[0])
        ring_copy(None, ref, parts, ssem, rsem, 4).start()
        got(ref.at[at_x(1), parts[1]], rsem.at[1])
        ring_copy(None, ref, parts, ssem, rsem, 5).start()

    def ring_rest(ref, rsem):
        got(ref.at[pl.ds(0, 2)], rsem.at[2])

    up_parts = (pl.ds(0, 8), pl.ds(8, 8))
    ft_parts = (pl.ds(0, half), pl.ds(half, half + 16))

    my_rows = w_out.at[pl.ds(pl.multiple_of(z * 32, 32), 32), :]

    def slice_send(d):
        return send(my_rows, sl.at[y], s_sl, r_sl, row_dev(at_y(d), c))

    def to_col(src, dst, ssem, rsem, d):
        return send(src, dst, ssem, rsem, {"col": at_x(d)})

    halo_start(0, image_hbm)
    for d in range(1, ny):
        slice_send(d).start()
    for n in range(4):
        ring_copy(up_hbm, ups, up_parts, s_up, r_up, n).start()
    for j in range(2):
        win_send(True, 0, j).start()
        win_send(False, 0, j).start()
        win_share(0, y, j).start()
    local = [
        pltpu.make_async_copy(w_in, win.at[r], s_loc.at[1]),
        pltpu.make_async_copy(my_rows, sl.at[y], s_loc.at[2]),
        pltpu.make_async_copy(up_hbm, ups.at[x], s_loc.at[3]),
    ]
    for copy in local:
        copy.start()
    for copy in loads:
        copy.wait()

    fill(pl.ds(3, 16), pl.ds(8, 16), image[...].astype(F32))
    halo_take(0)

    def keep(i, cols, value):
        mix[i, :, cols] = value

    g_row = gain[...]
    g_high = g_row.astype(BF16).astype(F32)
    tail = lax.broadcasted_iota(jnp.int32, (16, 256), 0)
    feat[x, pl.ds(cells, 16), :] = jnp.where(
        tail == 0, g_high, jnp.where(tail == 1, g_row - g_high, 0.0)
    ).astype(BF16)
    lane = lax.broadcasted_iota(jnp.int32, (half, 128), 1)

    def as_rows(first, second):
        both = jnp.where(lane == 0, first, jnp.where(lane == 1, second, 0.0))
        return both.T[0:8, :]

    stat_own = pl.ds(pl.multiple_of(x * 8, 8), 8)

    def centre_half(p):
        flat = mix[8 * p : 8 * p + 8].reshape(half, 256)
        mean_own = jnp.sum(flat, axis=-1, keepdims=True) * (1.0 / 256)
        centred = flat - mean_own
        square = jnp.sum(centred * centred, axis=-1, keepdims=True)
        feat[x, pl.ds(half * p, half), :] = (centred * g_row).astype(BF16)
        stat[stat_own, pl.ds(half * p, half)] = as_rows(mean_own, square)

    def feat_copy(n):
        return ring_copy(feat.at[x] if n < 4 else None, feat, ft_parts, s_ft, r_ft, n)

    def cross(d):
        dest = at_x(d)
        return send(
            sl.at[pl.ds(2 * dest, 2)], wo.at[x, :, c, z], s_wx, r_wx, {"col": dest}
        )

    others = nx - 1
    stat_bytes = stat.at[pl.ds(0, 8 * others), :]

    ring_relay(ups, up_parts, s_up, r_up)
    conv(False, 0, keep)
    centre_half(0)
    feat_copy(0).start()

    for copy in local:
        copy.wait()
    got(sl.at[pl.ds(0, ny - 1)], r_sl)
    for d in range(1, nx):
        cross(d).start()
    mine = pltpu.make_async_copy(sl.at[pl.ds(2 * x, 2)], wo.at[x, :, c, z], s_loc.at[4])
    mine.start()
    conv(False, 8, keep)
    centre_half(1)
    for d in range(1, nx):
        to_col(stat.at[stat_own, :], stat.at[stat_own, :], s_st, r_st, d).start()
    for n in (1, 2, 3):
        feat_copy(n).start()
    win_relay(1, 0)
    win_relay(1, 1)
    mine.wait()
    got(sl.at[pl.ds(0, 2 * others)], r_wx)
    for j in range(2):
        wo_send(True, 0, j).start()
        wo_send(False, 0, j).start()
        wo_share(0, z, j).start()
    win_relay(2, 0)
    ring_relay(feat, ft_parts, s_ft, r_ft)
    win_relay(2, 1)
    wo_relay(1, 0)
    win_relay(3, 0)
    wo_relay(1, 1)
    win_relay(3, 1)
    wo_relay(2, 0)
    win_relay(4, 0)
    wo_relay(2, 1)
    win_relay(4, 1)

    got(stat_bytes, r_st)
    ring_rest(feat, r_ft)
    got(win.at[pl.ds(0, ny)], r_wp)

    columns = stat[...].T
    means = [columns[:, 8 * k : 8 * k + 1] for k in range(nx)]
    centre = (means[0] + means[1] + means[2] + means[3]) * 0.25
    shifts = [m - centre for m in means]
    total = columns[:, 1:2] + columns[:, 9:10] + columns[:, 17:18] + columns[:, 25:26]
    spread = total + 256.0 * (
        shifts[0] * shifts[0] + shifts[1] * shifts[1] + shifts[2] * shifts[2]
        + shifts[3] * shifts[3]
    )
    inv_std = lax.rsqrt(spread * (1.0 / 1024) + EPSILON)
    for k in range(nx):
        dinv[k] = jnp.broadcast_to(shifts[k] * inv_std, (cells, 128))
    dinv[4] = jnp.broadcast_to(inv_std, (cells, 128))
    dinv[5] = jnp.broadcast_to(centre, (cells, 128))

    def wide(n):
        part = dinv[n]
        return jnp.concatenate([part, part], axis=1)

    def first_product(n, carry):
        cols = pl.ds(pl.multiple_of(n * 256, 256), 256)
        acc = jnp.zeros((cells, 256), F32)
        shift = jnp.zeros((cells, 256), F32)
        gsum = jnp.zeros((1, 256), F32)
        for k in range(nx):
            block = win[4 * k : 4 * k + 4, :, cols].reshape(256, 256)
            part = dot_nn(feat[k], block)
            acc = acc + part[:cells]
            row = part[cells : cells + 1] + part[cells + 1 : cells + 2]
            shift = shift + wide(k) * row
            gsum = gsum + row
        pre[:, cols] = acc * wide(4) + shift
        gws[:, cols] = jnp.broadcast_to(gsum, (8, 256))
        return carry

    lax.fori_loop(0, 2, first_product, 0)
    wo_relay(3, 0)
    lax.fori_loop(2, 4, first_product, 0)

    wo_relay(3, 1)
    for j in range(2):
        wo_relay(4, j)
    ring_rest(ups, r_up)
    got(win.at[pl.ds(0, nz)], r_zp)

    sums[...] = jnp.zeros(sums.shape, F32)

    def activation(n, carry):
        cols = pl.ds(pl.multiple_of(n * 256, 256), 256)
        grad = jnp.zeros((cells, 256), F32)
        for k in range(nx):
            block = wo[k, lax.div(n, 2), lax.rem(n, 2)].reshape(256, 256)
            grad = grad + dot_nt(ups[k].reshape(cells, 256), block)
        value = pre[:, cols]
        phi = 0.5 * (1.0 + lax.erf(value * (1.0 / math.sqrt(2.0))))
        slope = phi + value * jnp.exp(-0.5 * value * value) * (1.0 / math.sqrt(2.0 * math.pi))
        hb[:, cols] = (value * phi).astype(BF16)
        act = (grad * slope).astype(BF16)
        ag[:, cols] = act
        actf = act.astype(F32)
        one = actf * gws[0:1, cols]
        two = actf * value
        sums[0] += one[:, :128] + one[:, 128:]
        sums[1] += two[:, :128] + two[:, 128:]
        return carry

    lax.fori_loop(0, 4, activation, 0)

    def win_block(k):
        return win[pl.ds(pl.multiple_of(k * 4, 4), 4)].reshape(256, 1024)

    for p in range(2):
        rows_of = pl.ds(half * p, half)
        stat2[stat_own, rows_of] = as_rows(
            jnp.sum(sums[0, rows_of, :], axis=-1, keepdims=True),
            jnp.sum(sums[1, rows_of, :], axis=-1, keepdims=True),
        )
    for d in range(1, nx):
        to_col(stat2.at[stat_own, :], stat2.at[stat_own, :], s_s2, r_s2, d).start()

    class Scatter:
        def __init__(self, far, keep_f32, sent, far_got, got_, own, ssem, rsem, product):
            self.far, self.keep, self.sent = far, keep_f32, sent
            self.far_got, self.got, self.own = far_got, got_, own
            self.ssem, self.rsem, self.product = ssem, rsem, product

        def copy(self, n):
            to = right if n in (0, 2, 4) else left
            rows_ = pl.ds(half * (0, 1, 1, 0, 0, 1)[n], half)
            side = n % 2
            if n < 2:
                src, dst = self.far.at[rows_], self.far_got.at[side]
            else:
                src, dst = self.sent.at[side, rows_], self.got.at[side, rows_]
            return send(src, dst, self.ssem, self.rsem.at[min(n, 2)], to)

        def begin(self):
            self.far[...] = self.product(at_x(2)).astype(BF16)

        def near(self):
            value = self.product(at_x(1))
            self.keep[0] = value[:half]
            self.sent[0, half:] = value[half:].astype(BF16)

        def other(self):
            value = self.product(at_x(nx - 1))
            self.keep[1] = value[half:]
            self.sent[1, :half] = value[:half].astype(BF16)

        def relay(self):
            got(self.far_got.at[0], self.rsem.at[0])
            self.sent[0, :half] = (self.keep[0] + self.far_got[0].astype(F32)).astype(BF16)
            self.copy(4).start()
            got(self.far_got.at[1], self.rsem.at[1])
            self.sent[1, half:] = (self.keep[1] + self.far_got[1].astype(F32)).astype(BF16)
            self.copy(5).start()

        def total(self):
            got(self.got, self.rsem.at[2])
            return self.own[...] + self.got[0].astype(F32) + self.got[1].astype(F32)

    grads = Scatter(
        fg2, fgk, fgs, fge, fgr, fgo, s_fg, r_fg, lambda k: dot_nt(ag[...], win_block(k))
    )
    outs = Scatter(
        ob2, obk, obs, obe, obr, obo, s_ob, r_ob,
        lambda k: dot_nn(hb[...], wo[k].reshape(1024, 256)),
    )
    grads.begin()
    grads.copy(0).start()
    grads.copy(1).start()
    grads.near()
    grads.copy(2).start()
    grads.other()
    grads.copy(3).start()
    fgo[...] = grads.product(x)
    outs.begin()
    outs.near()
    outs.other()
    grads.relay()
    for n in range(4):
        outs.copy(n).start()
    obo[...] = outs.product(x)

    got(stat_bytes, r_s2)
    feature = grads.total()
    columns2 = stat2[...].T
    first = (
        columns2[:, 0:1] + columns2[:, 8:9] + columns2[:, 16:17] + columns2[:, 24:25]
    ) * (1.0 / 1024)
    second = (
        columns2[:, 1:2] + columns2[:, 9:10] + columns2[:, 17:18] + columns2[:, 25:26]
    ) * (1.0 / 1024)
    inv_wide = wide(4)
    normed = (mix[...].reshape(cells, 256) - wide(5)) * inv_wide
    mixed_grad = inv_wide * (feature * g_row - first - normed * second)
    mgb[...] = mixed_grad.astype(BF16).reshape(16, 16, 256)
    halo_start(1, mgb)
    fill(pl.ds(3, 16), pl.ds(8, 16), mixed_grad.reshape(16, 16, 256))
    outs.relay()
    halo_take(1)

    def finish(i, cols, value):
        igrad[i, :, cols] = ups[x, i, :, cols].astype(F32) + value

    conv(True, 0, finish)
    conv(True, 8, finish)
    out[...] = (image[...].astype(F32) + outs.total().reshape(16, 16, 256)).astype(BF16)

    for p in range(2):
        left_here(halo_bytes, s_halo.at[p])
    left_here(win.at[pl.ds(0, 2 * ny - 1)], s_w)
    left_here(win.at[pl.ds(0, 2 * nz - 1)], s_z)
    left_here(sl.at[pl.ds(0, ny - 1)], s_sl)
    left_here(sl.at[pl.ds(0, 2 * others)], s_wx)
    left_here(ups.at[pl.ds(0, 3)], s_up)
    left_here(feat.at[pl.ds(0, 3)], s_ft)
    for ssem in (s_fg, s_ob):
        left_here(ups.at[pl.ds(0, 3)], ssem)
    for ssem in (s_st, s_s2):
        left_here(stat_bytes, ssem)


def local(image, conv_kernel, norm_gain, w_in, w_out, upstream):
    nz, nr, nx = lax.axis_size("section"), lax.axis_size("row"), lax.axis_size("col")
    ny = nr // 2
    height, breadth, chan = image.shape
    cells = height * breadth
    vmem = pl.BlockSpec(memory_space=pltpu.VMEM)
    dma = pltpu.SemaphoreType.DMA
    any_ = pl.BlockSpec(memory_space=pl.ANY)
    half = cells // 2
    scatter = [
        pltpu.VMEM((cells, chan), BF16),
        pltpu.VMEM((2, half, chan), F32),
        pltpu.VMEM((2, cells, chan), BF16),
        pltpu.VMEM((2, half, chan), BF16),
        pltpu.VMEM((2, cells, chan), BF16),
        pltpu.VMEM((cells, chan), F32),
    ]
    scratch = [
        pltpu.VMEM((height, breadth, chan), BF16),
        pltpu.VMEM((7, 7, chan), F32),
        pltpu.VMEM((1, chan), F32),
        pltpu.VMEM((2, 2, 16, EDGE, chan), BF16),
        pltpu.VMEM((2, 2, 3, 16, chan), BF16),
        pltpu.VMEM((2, 4, 3, EDGE, chan), BF16),
        pltpu.VMEM((2, 22, 32, 128), F32),
        pltpu.VMEM((height, breadth, chan), F32),
        pltpu.VMEM((nx, cells + 16, chan), BF16),
        pltpu.VMEM((128, cells), F32),
        pltpu.VMEM((128, cells), F32),
        pltpu.VMEM((nx, height, breadth, chan), BF16),
        pltpu.VMEM((nr, 64, 1024), BF16),
        pltpu.VMEM((ny, 32, chan), BF16),
        pltpu.VMEM((nx, 2, 2, nz, 32, chan), BF16),
        pltpu.VMEM((cells, 1024), F32),
        pltpu.VMEM((8, 1024), F32),
        pltpu.VMEM((cells, 1024), BF16),
        pltpu.VMEM((cells, 1024), BF16),
        pltpu.VMEM((2, cells, 128), F32),
        *scatter,
        *scatter,
        pltpu.VMEM((height, breadth, chan), BF16),
        pltpu.VMEM((6, cells, 128), F32),
        dma((2,)), dma((2,)),
        dma, dma((3,)),
        dma, dma,
        dma, dma((3,)),
        dma, dma((nr, 2)), dma,
        dma, dma,
        dma, dma,
        dma, dma((nz, 2)), dma,
        dma, dma((3,)),
        dma, dma,
        dma, dma((3,)),
        dma((8,)),
    ]
    return pl.pallas_call(
        body,
        out_shape=(
            pltpu.VMEM(image.shape, BF16),
            pltpu.VMEM(image.shape, F32),
        ),
        in_specs=[any_] * 6,
        out_specs=(vmem, vmem),
        scratch_shapes=scratch,
        compiler_params=pltpu.CompilerParams(
            collective_id=0, has_side_effects=True, vmem_limit_bytes=60 * 1024 * 1024
        ),
        name="block",
    )(image, conv_kernel, norm_gain.reshape(1, chan), w_in, w_out, upstream)


def solution(mesh):
    in_specs = (
        P("section", "row", "col"),
        P(None, None, "col"),
        P("col"),
        P("row", "col"),
        P("row", "col"),
        P("section", "row", "col"),
    )
    out_specs = (P("section", "row", "col"), P("section", "row", "col"))
    return jax.shard_map(local, mesh=mesh, in_specs=in_specs, out_specs=out_specs, check_vma=False)
```
